32 devices in a mesh: member: 4 (over z), region: 8 (over y, x, core).
Axes of the slice: x: 2, y: 2, z: 4, core: 2. Of those that a mesh axis runs over, the one named last changes fastest.
Arguments:
- background: bfloat16 [64, 13, 192, 1024], P('member', None, 'region'), may hold values from -6 to 6
- obs_ens: bfloat16 [131072, 64], P(('member', 'region')), may hold values from -6 to 6
- obs_value: bfloat16 [131072], P(('member', 'region')), may hold values from -8 to 8
- obs_precision: bfloat16 [131072], P(('member', 'region')), may hold values from 0.0009994507 to 0.0099487305
- obs_row: int32 [131072], P(('member', 'region')), may hold values from 0 to 47
- obs_patch: int32 [131072, 1], P(('member', 'region')), may hold values from 0 to 31; in each aligned block of 4096 rows (0 to 4095, 4096 to 8191, ...) at most 256 rows name the same one
Outputs:
- analysis: bfloat16 [64, 13, 192, 1024], P(None, None, 'member', 'region')
The draws below stay inside these ranges and needn't reach their ends.
Inputs may be any that keep to these rules, and one draw needn't show every extreme that they name: `obs_patch`: among the observations of one device, at most 256 fall in one patch, and some patch receives exactly 256 of them.
All inputs are finite; a program needn't handle non-finite values.
Results may differ from the reference program's by a relative error of at most 0.0015.
The reference program's roundings to bfloat16 on the way count: a program that leaves them out, or rounds other values in their place, can miss the bound.
Values may be sent and summed in bfloat16 or wider, within the bound.
A program may use at most 128 MiB of HBM per device.

```python
import math
import jax
import jax.numpy as jnp
import numpy as np
from jax import lax

K = 64
C = 13
PLAT = 48
PLON = 128
BAND = 2
OBS_DEV = 4096
NS_ITERS = 4
CAP = 256
NPATCH = 32
NLAT = 192
NLON = 1024
NOBS = 131072
N_MEMBER = 4
N_REGION = 8


def place_ends(array, key, low, high):
    place = [jax.random.randint(jax.random.fold_in(key, axis), (), 0, length) for axis, length in enumerate(array.shape)]
    widest = array.shape.index(max(array.shape))
    next_to = place[:widest] + [(place[widest] + 1) % array.shape[widest]] + place[widest + 1:]
    return array.at[tuple(place)].set(low).at[tuple(next_to)].set(high)


def levels(rng, extent, split, smallest, high):
    def one(dim, parts):
        draws = jax.random.uniform(jax.random.fold_in(jax.random.fold_in(rng, 6), dim), (parts,), jnp.float32, smallest / len(split), high / len(split))
        return jnp.repeat(jnp.exp(draws), extent[dim] // parts).reshape((-1,) + (1,) * (len(extent) - dim - 1))

    gain = one(*split[0])
    for cut in split[1:]:
        gain = gain * one(*cut)
    return gain


def assign_block(own_key, own, number, rows, count, top, bound, lean):
    sequence = jax.random.permutation(own_key, count)
    packed, ordinary = shares(count, rows * top, bound, lean, True), shares(count, rows * top, bound, lean, False)
    places = jnp.arange(count)

    def named(tallies, turn):
        used = int((tallies > 0).sum())
        fixed = max(1, used // 4)
        moved = fixed + (places - fixed + turn * (used - fixed)) % max(1, count - fixed)
        return jnp.zeros((count,), jnp.int32).at[sequence[jnp.where(places < fixed, places, moved)]].set(jnp.asarray(tallies, jnp.int32))

    tallies = jnp.where(number % 4 == 0, named(packed, number // 4), named(ordinary, number - number // 4 - 1))
    mixed = jax.random.permutation(jax.random.fold_in(own, 3), count)
    source_of, sink = mixed[0:count // 2 * 2:2], mixed[1:count // 2 * 2:2]
    margin = jnp.minimum(tallies[source_of] - 1, bound - tallies[sink]) // 2
    margin = jnp.where((source_of == sequence[0]) | (sink == sequence[0]) | (tallies[sink] == 0), 0, jnp.maximum(margin, 0))
    moved = jax.random.randint(jax.random.fold_in(own, 4), (count // 2,), 0, 1 << 20) % (margin + 1)
    tallies = tallies.at[source_of].add(-moved).at[sink].add(moved)
    members = jnp.searchsorted(jnp.cumsum(tallies), jnp.arange(rows * top), side="right").astype(jnp.int32)
    table = members.reshape(top, rows).T
    table = table[jax.random.permutation(jax.random.fold_in(own, 1), rows)]
    turn = jax.random.randint(jax.random.fold_in(own, 2), (rows, 1), 0, top)
    return jnp.take_along_axis(table, (jnp.arange(top)[None, :] + turn) % top, axis=1)


def shares(number_of, total, bound, skew, full):
    weights = [(1 << 20) // math.isqrt(grade ** skew) + 1 for grade in range(1, number_of + 1)]
    largest = bound if full else min(bound, max(-(-total // number_of), total * weights[0] // sum(weights)))
    least = 1 if total - largest >= number_of - 1 else 0
    given, rest = [largest] + [least] * (number_of - 1), total - largest - least * (number_of - 1)
    while rest > 0:
        candidates = [i for i in range(1, number_of) if given[i] < largest] or [i for i in range(1, number_of) if given[i] < bound]
        pool, left = sum([weights[i] for i in candidates]), rest
        for i in candidates:
            more = min(bound - given[i], max(1, left * weights[i] // pool), rest)
            given[i] = given[i] + more
            rest = rest - more
    return np.array(given)


def centred(own_key, extent, deviation, most, split=(), kind=jnp.bfloat16):
    gain = levels(own_key, extent, split, -0.22, 0.18) if split else 1.0
    values = jax.random.normal(own_key, extent, jnp.float32) * deviation * gain
    return jnp.minimum(jnp.maximum(values, -most), most).astype(kind)


def setup_inputs(seed: int = 0) -> dict:
    key_list = jax.random.split(jax.random.key(seed), 7)
    background = centred(key_list[0], (K, C, NLAT, NLON), 1.0, 6.0, ((0, 4), (2, 8)))
    obs_ens = centred(key_list[1], (NOBS, K), 1.0, 6.0, ((0, 32),))
    obs_value = centred(key_list[2], (NOBS,), 2.0, 8.0, ((0, 32),))
    obs_precision = jnp.clip(jnp.exp(math.log(0.0099487305) - 2.2979944 * jax.random.uniform(key_list[3], (NOBS,), jnp.float32) ** levels(key_list[3], (NOBS,), ((0, 32),), -0.2, 0.2)), 0.0009994507, 0.0099487305).astype(jnp.bfloat16)
    obs_row = place_ends(jax.random.randint(key_list[4], (NOBS,), 0, PLAT), jax.random.fold_in(key_list[4], 1), 0, PLAT - 1).astype(jnp.int32)
    obs_patch_keys = jax.random.split(jax.random.fold_in(key_list[5], 1), NOBS // OBS_DEV)
    obs_patch_turns = jax.random.permutation(jax.random.fold_in(key_list[5], 3), NOBS // OBS_DEV)
    obs_patch = jax.vmap(lambda own, number: assign_block(jax.random.fold_in(key_list[5], 2), own, number, OBS_DEV, NPATCH, 1, CAP, 1))(obs_patch_keys, obs_patch_turns).reshape((NOBS, 1))
    return {"background": background, "obs_ens": obs_ens, "obs_value": obs_value, "obs_precision": obs_precision, "obs_row": obs_row, "obs_patch": obs_patch}


def batched(left, right):
    return jnp.einsum('bij,bjk->bik', left, right, precision=lax.Precision.HIGHEST)

def localize(row_float, obs_prec):
    centers = jnp.arange(PLAT // BAND, dtype=jnp.float32) * BAND + (BAND - 1) / 2.0
    distance = (row_float[None, :] - centers[:, None]) / (PLAT / 4.0)
    return obs_prec[None, :] * jnp.exp(-0.5 * distance * distance)

def band_transforms(ens_vals, obs_val, obs_prec, row_float):
    ens_float = ens_vals.astype(jnp.float32)
    ens_mean = lax.optimization_barrier(jnp.sum(ens_float, axis=1)) / K
    ens_pert = (ens_float - ens_mean[:, None]).astype(jnp.bfloat16)
    pert_float = ens_pert.astype(jnp.float32)
    innovation = obs_val - ens_mean
    weight = localize(row_float, obs_prec)

    def band_gram(band_weight):
        scaled = (band_weight[:, None] * pert_float).astype(jnp.bfloat16)
        return lax.dot_general(scaled, ens_pert, (((0,), (0,)), ((), ())), preferred_element_type=jnp.float32)
    gram_band = lax.map(band_gram, weight)
    projected = jnp.dot(weight * innovation[None, :], pert_float, precision=lax.Precision.HIGHEST)
    identity = jnp.eye(K, dtype=jnp.float32)
    system = (K - 1.0) * identity + gram_band
    norm_f = jnp.sqrt(lax.optimization_barrier(jnp.sum(system * system, axis=(1, 2))))
    root_iter = system / norm_f[:, None, None]
    inv_root = jnp.broadcast_to(identity, system.shape)
    for newton_step in range(NS_ITERS):
        middle = 1.5 * identity - 0.5 * batched(inv_root, root_iter)
        root_iter = batched(root_iter, middle)
        inv_root = batched(middle, inv_root)
    spread = jnp.sqrt((K - 1.0) / norm_f)[:, None, None] * inv_root
    inverse = batched(inv_root, inv_root) / norm_f[:, None, None]
    mean_shift = jnp.einsum('bjk,bk->bj', inverse, projected, precision=lax.Precision.HIGHEST)
    return (spread + mean_shift[:, :, None]).astype(jnp.bfloat16)

def update(patch_states, transform):
    state_mean = lax.optimization_barrier(jnp.sum(patch_states.astype(jnp.float32), axis=0)) / K
    state_pert = (patch_states.astype(jnp.float32) - state_mean[None]).astype(jnp.bfloat16)
    shaped = state_pert.reshape(K, C, PLAT // BAND, BAND, PLON).astype(jnp.float32)
    increment = jnp.einsum('jcbxl,bjk->kcbxl', shaped, transform.astype(jnp.float32))
    result = state_mean.reshape(1, C, PLAT // BAND, BAND, PLON) + increment
    return result.reshape(K, C, PLAT, PLON).astype(jnp.bfloat16)

def reference(background, obs_ens, obs_value, obs_precision, obs_row, obs_patch):
    target_patch = obs_patch[:, 0].astype(jnp.int32)
    ordering = jnp.argsort(target_patch, stable=True).astype(jnp.int32)
    counts = jax.ops.segment_sum(jnp.ones_like(target_patch), target_patch, NPATCH).astype(jnp.int32)
    starts = (jnp.cumsum(counts) - counts).astype(jnp.int32)
    room = NPATCH * CAP
    padded_order = jnp.concatenate([ordering, jnp.zeros((room,), jnp.int32)])

    def one_patch(patch_id):
        picked = lax.dynamic_slice_in_dim(padded_order, starts[patch_id], room)
        is_live = jnp.arange(room, dtype=jnp.int32) < counts[patch_id]
        ens_vals = jnp.where(is_live[:, None], obs_ens[picked], jnp.zeros((), jnp.bfloat16))
        obs_val = jnp.where(is_live, obs_value[picked].astype(jnp.float32), 0.0)
        obs_prec = jnp.where(is_live, obs_precision[picked].astype(jnp.float32), 0.0)
        row_float = obs_row[picked].astype(jnp.float32)
        transform = band_transforms(ens_vals, obs_val, obs_prec, row_float)
        lat_block = (patch_id // N_REGION).astype(jnp.int32)
        lon_block = (patch_id % N_REGION).astype(jnp.int32)
        zero = jnp.zeros((), jnp.int32)
        patch_states = lax.dynamic_slice(background, (zero, zero, lat_block * PLAT, lon_block * PLON), (K, C, PLAT, PLON))
        return update(patch_states, transform)
    patches = lax.map(one_patch, jnp.arange(NPATCH, dtype=jnp.int32))
    patches = patches.reshape(N_MEMBER, N_REGION, K, C, PLAT, PLON)
    return patches.transpose(2, 3, 0, 4, 1, 5).reshape(K, C, NLAT, NLON)
```

```python
import functools
import math

import jax
import jax.numpy as jnp
from jax import lax
from jax.experimental import pallas as pl
from jax.experimental.pallas import tpu as pltpu
from jax.sharding import PartitionSpec as P


BAND = 2
NS_ITERS = 4
PIECES = 4


def batched(left, right):
    return jnp.einsum("bij,bjk->bik", left, right, precision=lax.Precision.HIGHEST)


def gram_kernel(width, lat_rows, recv_ref, gram_ref, proj_ref, scaled_ref):
    bands = lat_rows // BAND

    @pl.when(pl.program_id(0) == 0)
    def _():
        gram_ref[...] = jnp.zeros_like(gram_ref)
        proj_ref[...] = jnp.zeros_like(proj_ref)

    cols = recv_ref[...].astype(jnp.float32).T
    ens = cols[:width]
    obs_val, obs_prec, row = (cols[width + k : width + k + 1] for k in range(3))
    mean = jnp.sum(ens, axis=0, keepdims=True) / width
    pert = (ens - mean).astype(jnp.bfloat16)
    pert_float = pert.astype(jnp.float32)
    innovation = obs_val - mean
    index = lax.broadcasted_iota(jnp.int32, (bands, 1), 0).astype(jnp.float32)
    distance = (row - (index * BAND + (BAND - 1) / 2.0)) / (lat_rows / 4.0)
    weight = obs_prec * jnp.exp(-0.5 * distance * distance)
    for j in range(bands):
        scaled_ref[j * width : (j + 1) * width, :] = (weight[j : j + 1] * pert_float).astype(
            jnp.bfloat16
        )
    over_obs = (((1,), (1,)), ((), ()))
    gram_ref[...] += lax.dot_general(
        scaled_ref[...], pert, over_obs, preferred_element_type=jnp.float32
    )
    proj_ref[...] += lax.dot_general(
        weight * innovation,
        pert_float,
        over_obs,
        precision=lax.Precision.HIGHEST,
        preferred_element_type=jnp.float32,
    )


def band_grams(recv, width, lat_rows):
    slots, cols = recv.shape
    bands = lat_rows // BAND
    block = math.gcd(slots, 1024)
    gram, projected = pl.pallas_call(
        functools.partial(gram_kernel, width, lat_rows),
        grid=(slots // block,),
        in_specs=[pl.BlockSpec((block, cols), lambda i: (i, 0))],
        out_specs=[
            pl.BlockSpec((bands * width, width), lambda i: (0, 0)),
            pl.BlockSpec((bands, width), lambda i: (0, 0)),
        ],
        out_shape=[
            jax.ShapeDtypeStruct((bands * width, width), jnp.float32),
            jax.ShapeDtypeStruct((bands, width), jnp.float32),
        ],
        scratch_shapes=[pltpu.VMEM((bands * width, block), jnp.bfloat16)],
        compiler_params=pltpu.CompilerParams(vmem_limit_bytes=24 << 20),
        cost_estimate=pl.CostEstimate(
            flops=8 * slots * bands * width * width,
            bytes_accessed=2 * slots * cols,
            transcendentals=slots * bands,
        ),
    )(recv)
    return gram.reshape(bands, width, width), projected


def batched(left, right):
    return jnp.einsum("bij,bjk->bik", left, right, precision=lax.Precision.HIGHEST)


def band_transforms(grams, members):
    gram_band, projected = grams
    identity = jnp.eye(members, dtype=jnp.float32)
    system = (members - 1.0) * identity + gram_band
    norm_f = jnp.sqrt(jnp.sum(system * system, axis=(1, 2)))
    root_iter = system / norm_f[:, None, None]
    inv_root = jnp.broadcast_to(identity, system.shape)
    for _ in range(NS_ITERS):
        middle = 1.5 * identity - 0.5 * batched(inv_root, root_iter)
        root_iter = batched(root_iter, middle)
        inv_root = batched(middle, inv_root)
    spread = jnp.sqrt((members - 1.0) / norm_f)[:, None, None] * inv_root
    inverse = batched(inv_root, inv_root) / norm_f[:, None, None]
    mean_shift = jnp.einsum("bjk,bk->bj", inverse, projected, precision=lax.Precision.HIGHEST)
    return (spread + mean_shift[:, :, None]).astype(jnp.bfloat16)


def slot_numbers(target_patch, devices, capacity):
    obs_rows = target_patch.shape[0]
    block = math.gcd(obs_rows, 512)
    nblock = obs_rows // block
    onehot = (target_patch[:, None] == jnp.arange(devices, dtype=jnp.int32)[None, :]).astype(
        jnp.bfloat16
    )
    blocks = onehot.reshape(nblock, block, devices)
    lower = (jnp.arange(block)[:, None] > jnp.arange(block)[None, :]).astype(jnp.bfloat16)
    inner = jnp.einsum("ij,bjd->bid", lower, blocks, preferred_element_type=jnp.float32)
    totals = jnp.sum(blocks, axis=1, dtype=jnp.float32)
    offsets = jnp.cumsum(totals, axis=0) - totals
    before = inner + offsets[:, None, :]
    rank = jnp.sum(before * blocks.astype(jnp.float32), axis=2).reshape(obs_rows).astype(jnp.int32)
    return target_patch * capacity + rank


def dispatch_kernel(slots_ref, packed_ref, out_ref, wide_ref):
    obs_rows = packed_ref.shape[0]
    wide_ref[...] = jnp.zeros_like(wide_ref)
    unroll = math.gcd(obs_rows, 16)

    def place(step, carry):
        for k in range(unroll):
            i = step * unroll + k
            wide_ref[pl.ds(slots_ref[i], 1), :] = packed_ref[pl.ds(i, 1), :]
        return carry

    lax.fori_loop(0, obs_rows // unroll, place, 0)
    out_ref[...] = wide_ref[...].astype(jnp.bfloat16)


def dispatch(slots, packed, total_slots):
    obs_rows, cols = packed.shape
    return pl.pallas_call(
        dispatch_kernel,
        in_specs=[
            pl.BlockSpec(memory_space=pltpu.SMEM),
            pl.BlockSpec(memory_space=pltpu.VMEM),
        ],
        out_specs=pl.BlockSpec(memory_space=pltpu.VMEM),
        out_shape=jax.ShapeDtypeStruct((total_slots, cols), jnp.bfloat16),
        scratch_shapes=[pltpu.VMEM((total_slots, cols), jnp.float32)],
        compiler_params=pltpu.CompilerParams(vmem_limit_bytes=24 << 20),
        cost_estimate=pl.CostEstimate(
            flops=1 << 32, bytes_accessed=8 * obs_rows * cols, transcendentals=0
        ),
    )(slots, packed)


def scatter_step(spread, shift, strips_each):
    members = lax.axis_size("member")
    target = lax.rem(lax.axis_index("member") + shift, members)
    block = lax.dynamic_slice_in_dim(spread, target * strips_each, strips_each, axis=0)
    if shift == 0:
        return block
    ring = [(k, (k + shift) % members) for k in range(members)]
    return lax.ppermute(block, "member", ring)


def local(background, obs_ens, obs_value, obs_precision, obs_row, obs_patch):
    members = lax.axis_size("member")
    regions = lax.axis_size("region")
    devices = members * regions
    obs_rows = obs_row.shape[0]
    capacity = 2 * obs_rows // devices
    total_slots = devices * capacity
    width = obs_ens.shape[1]
    target_patch = obs_patch[:, 0]
    slots = slot_numbers(target_patch, devices, capacity)
    packed_cols = (width + 3 + 127) // 128 * 128
    extras = jnp.stack([obs_value, obs_precision, obs_row.astype(jnp.bfloat16)], axis=1)
    filler = jnp.zeros((obs_rows, packed_cols - width - 3), jnp.bfloat16)
    packed = jnp.concatenate([obs_ens, extras, filler], axis=1)
    buffer = dispatch(slots, packed.astype(jnp.float32), total_slots)
    local_members = background.shape[0]
    channels = background.shape[1]
    rows_local = background.shape[2]
    lon_cols = background.shape[3] // regions
    strips_each = regions // members
    lat_rows = strips_each * rows_local
    edges = [channels * k // PIECES for k in range(PIECES + 1)]

    def analyse(piece, row_transform):
        patch_states = jnp.stack(piece)
        state_mean = jnp.sum(patch_states, axis=(0, 2), dtype=jnp.float32) / width
        state_pert = (
            patch_states.astype(jnp.float32) - jnp.expand_dims(state_mean, (0, 2))
        ).astype(jnp.bfloat16)
        increment = jnp.einsum(
            "mrjcxl,rxmjk->kcrxl", state_pert, row_transform, preferred_element_type=jnp.float32
        )
        result = state_mean.transpose(1, 0, 2, 3)[None] + increment
        return result.reshape(width, -1, lat_rows, lon_cols).astype(jnp.bfloat16)

    arrived = []
    results = []
    for k in range(PIECES):
        low, high = edges[k], edges[k + 1]
        states = background[:, low:high]
        if k == 1:
            states, recv = lax.optimization_barrier((states, recv))
        elif k == 2:
            states, grams = lax.optimization_barrier((states, grams))
        elif k == 3:
            states, row_transform = lax.optimization_barrier((states, row_transform))
        prepared = states.reshape(
            local_members, high - low, rows_local, regions, lon_cols
        ).transpose(3, 0, 1, 2, 4)
        spread = lax.all_to_all(prepared, "region", split_axis=0, concat_axis=0, tiled=True)
        if k == 0:
            spread, buffer = lax.optimization_barrier((spread, buffer))
            recv = lax.all_to_all(
                buffer, ("member", "region"), split_axis=0, concat_axis=0, tiled=True
            )
            spread, recv = lax.optimization_barrier((spread, recv))
        elif k == 1:
            grams = band_grams(recv, width, lat_rows)
        elif k == 2:
            transform = band_transforms(grams, width)
            row_transform = jnp.repeat(transform, BAND, axis=0).reshape(
                strips_each, rows_local, members, local_members, width
            )
            sources = (lax.axis_index("member") - jnp.arange(members) + members) % members
            row_transform = jnp.take(row_transform, sources, axis=2)
        elif k == 3:
            results = [analyse(piece, row_transform) for piece in arrived[:2]]
            spread, results = lax.optimization_barrier((spread, results))
        arrived.append([])
        for shift in range(members):
            arrived[k].append(scatter_step(spread, shift, strips_each))
    for k in range(2, PIECES):
        results.append(analyse(arrived[k], row_transform))
    return jnp.concatenate(results, axis=1)


def solution(mesh):
    in_specs = (
        P("member", None, "region", None),
        P(("member", "region"), None),
        P(("member", "region")),
        P(("member", "region")),
        P(("member", "region")),
        P(("member", "region"), None),
    )
    out_specs = P(None, None, "member", "region")
    return jax.shard_map(local, mesh=mesh, in_specs=in_specs, out_specs=out_specs, check_vma=False)
```
